32 devices in a mesh: rep: 4 (over x, core), fsdp: 8 (over z, y).
Axes of the slice: x: 2, y: 2, z: 4, core: 2. Of those that a mesh axis runs over, the one named last changes fastest.
Arguments:
- tokens: bfloat16 [2, 18432, 1024], P(None, ('rep', 'fsdp')), may hold values from -6 to 6
- out_grad: bfloat16 [2, 18432, 1024], P(None, ('rep', 'fsdp')), may hold values from -6 to 6
- image_starts: int32 [2, 4, 6], P(None, 'rep'), may hold values from 0 to 4031, as said below
- first_gain: bfloat16 [1024], P('fsdp'), may hold values from 0.5 to 1.5
- first_shift: bfloat16 [1024], P('fsdp'), may hold values from -1.5 to 1.5
- qkv_weight: bfloat16 [1024, 3072], P('fsdp'), may hold values from -0.1875 to 0.1875
- query_bias: bfloat16 [1024], P('fsdp'), may hold values from -1.5 to 1.5
- value_bias: bfloat16 [1024], P('fsdp'), may hold values from -1.5 to 1.5
- out_weight: bfloat16 [1024, 1024], P('fsdp'), may hold values from -1 to 1
- out_bias: bfloat16 [1024], P('fsdp'), may hold values from -1.5 to 1.5
- second_gain: bfloat16 [1024], P('fsdp'), may hold values from 0.5 to 1.5
- second_shift: bfloat16 [1024], P('fsdp'), may hold values from -1.5 to 1.5
- up_weight: bfloat16 [1024, 4096], P('fsdp'), may hold values from -0.1875 to 0.1875
- up_bias: bfloat16 [4096], P('fsdp'), may hold values from -1.5 to 1.5
- down_weight: bfloat16 [4096, 1024], P('fsdp'), may hold values from -0.09375 to 0.09375
- down_bias: bfloat16 [1024], P('fsdp'), may hold values from -1.5 to 1.5
Outputs:
- layer_out: bfloat16 [2, 18432, 1024], P(None, ('rep', 'fsdp'))
- tokens_grad: bfloat16 [2, 18432, 1024], P(None, ('rep', 'fsdp'))
- first_gain_grad: float32 [1024], P('fsdp')
- first_shift_grad: float32 [1024], P('fsdp')
- qkv_weight_grad: float32 [1024, 3072], P('fsdp')
- query_bias_grad: float32 [1024], P('fsdp')
- value_bias_grad: float32 [1024], P('fsdp')
- out_weight_grad: float32 [1024, 1024], P('fsdp')
- out_bias_grad: float32 [1024], P('fsdp')
- second_gain_grad: float32 [1024], P('fsdp')
- second_shift_grad: float32 [1024], P('fsdp')
- up_weight_grad: float32 [1024, 4096], P('fsdp')
- up_bias_grad: float32 [4096], P('fsdp')
- down_weight_grad: float32 [4096, 1024], P('fsdp')
- down_bias_grad: float32 [1024], P('fsdp')
The draws below stay inside these ranges and needn't reach their ends.
Inputs may be any that keep to these rules, and one draw needn't show every extreme that they name: `image_starts`: for each micro-batch and replica group, 6 image starts in rising order within the group's 8 * 576 packed positions; each image's 577 tokens end at or before the next image's start and within the group's positions. The first image starts at 0 and the last ends at the last position; positions in no image are padding.
All inputs are finite; a program needn't handle non-finite values.
Results may differ from the reference program's by a relative error of at most 0.015.
Values may be sent and summed in bfloat16 or wider, within the bound.
A program may use at most 320 MiB of HBM per device.

```python
import jax
import jax.numpy as jnp
from jax import lax

D = 1024
H = 16
HD = 64
FF = 4096
IMG = 577
MICRO = 2
MB_TOK = 576
IMGS = 6
TOKENS = 18432
N_REP = 4
N_FSDP = 8


def draw_image_starts(key, part):
    spare = N_FSDP * MB_TOK - IMGS * IMG
    raw_gaps = jax.random.randint(key, (MICRO, N_REP, IMGS), 0, spare + 1)
    sorted_gaps = jnp.sort(raw_gaps, axis=-1)
    sorted_gaps = sorted_gaps.at[:, :, 0].set(0)
    sorted_gaps = sorted_gaps.at[:, :, IMGS - 1].set(spare)
    offsets = IMG * jnp.arange(IMGS, dtype=jnp.int32)
    return (sorted_gaps + offsets[None, None, :]).astype(jnp.int32)


def block_levels(stream_key, dims, cuts, low, high):
    def one(dim, parts):
        draws = jax.random.uniform(jax.random.fold_in(jax.random.fold_in(stream_key, 6), dim), (parts,), jnp.float32, low / len(cuts), high / len(cuts))
        return jnp.repeat(jnp.exp(draws), dims[dim] // parts).reshape((-1,) + (1,) * (len(dims) - dim - 1))

    level = one(*cuts[0])
    for cut in cuts[1:]:
        level = level * one(*cut)
    return level


def centred(own_key, dims, width, most, pieces=(), kind=jnp.bfloat16):
    drawn = jax.random.normal(own_key, dims, jnp.float32) * width
    if len(pieces) > 0:
        drawn = block_levels(own_key, dims, pieces, -0.22, 0.18) * drawn
    return jnp.clip(drawn, min=-most, max=most).astype(kind)


def setup_inputs(seed: int = 0) -> dict:
    key_of = jax.random.split(jax.random.key(seed), 17)
    return {
        "tokens": centred(key_of[0], (MICRO, TOKENS, D), 1.0, 6.0, ((1, 32),)),
        "out_grad": centred(key_of[1], (MICRO, TOKENS, D), 1.0, 6.0, ((1, 32),)),
        "image_starts": draw_image_starts(jax.random.fold_in(key_of[16], 71), 0),
        "first_gain": jnp.clip(1.0 + 0.1 * jax.random.normal(key_of[3], (D,), jnp.float32), 0.5, 1.5).astype(jnp.bfloat16),
        "first_shift": centred(key_of[4], (D,), 0.3, 1.5, ((0, 8),)),
        "qkv_weight": centred(key_of[5], (D, 3 * D), D ** -0.5, 0.1875, ((0, 8),)),
        "query_bias": centred(key_of[6], (D,), 0.3, 1.5, ((0, 8),)),
        "value_bias": centred(key_of[7], (D,), 0.3, 1.5, ((0, 8),)),
        "out_weight": centred(key_of[8], (D, D), (max(8, D // 24)) ** -0.5, 1.0, ((0, 8),)),
        "out_bias": centred(key_of[9], (D,), 0.3, 1.5, ((0, 8),)),
        "second_gain": jnp.clip(1.0 + 0.1 * jax.random.normal(key_of[10], (D,), jnp.float32), 0.5, 1.5).astype(jnp.bfloat16),
        "second_shift": centred(key_of[11], (D,), 0.3, 1.5, ((0, 8),)),
        "up_weight": centred(key_of[12], (D, FF), D ** -0.5, 0.1875, ((0, 8),)),
        "up_bias": centred(key_of[13], (FF,), 0.3, 1.5, ((0, 8),)),
        "down_weight": centred(key_of[14], (FF, D), FF ** -0.5, 0.09375, ((0, 8),)),
        "down_bias": centred(key_of[15], (D,), 0.3, 1.5, ((0, 8),)),
    }


@jax.custom_vjp
def low(v):
    return lax.optimization_barrier(v.astype(jnp.bfloat16)).astype(jnp.float32)

@jax.custom_vjp
def low_back(v):
    return v

def low_keep(v):
    return (low(v), None)

def low_pass(kept, grad):
    return (grad,)

def back_keep(v):
    return (v, None)

def back_low(kept, grad):
    return (low(grad),)
low.defvjp(low_keep, low_pass)
low_back.defvjp(back_keep, back_low)
epsilon = 1e-06
highest = lax.Precision.HIGHEST
masked_score = -1e+30

def matmul(left, right):
    return jnp.dot(left, right, precision=highest, preferred_element_type=jnp.float32)

def norm_rows(values, gain, shift):
    centre = values - lax.optimization_barrier(jnp.mean(values, axis=-1, keepdims=True))
    spread = lax.optimization_barrier(jnp.mean(centre * centre, axis=-1, keepdims=True))
    return centre * lax.rsqrt(spread + epsilon) * gain + shift

def label_rows(places, starts):
    after = starts[None, :] <= places[:, None]
    inside = after & (places[:, None] < starts[None, :] + IMG)
    counted = lax.optimization_barrier(jnp.sum(after.astype(jnp.int32), axis=1)) - 1
    return jnp.where(jnp.any(inside, axis=1), counted, -1)

def allowed(query_start, width_rows, starts):
    query_place = query_start + jnp.arange(width_rows, dtype=jnp.int32)
    key_place = query_start - width_rows + jnp.arange(3 * width_rows, dtype=jnp.int32)
    query_label = label_rows(query_place, starts)
    key_label = label_rows(key_place, starts)
    same_image = (query_label[:, None] == key_label[None, :]) & (query_label[:, None] >= 0)
    return same_image | (query_place[:, None] == key_place[None, :])

def attend_block(block_index, queries, key_pad, value_pad, starts):
    width_rows = MB_TOK
    query_start = (block_index * width_rows).astype(jnp.int32)
    query_rows = lax.dynamic_slice_in_dim(queries, query_start, width_rows, 0).reshape(width_rows, H, HD)
    key_rows = lax.dynamic_slice_in_dim(key_pad, query_start, 3 * width_rows, 0).reshape(3 * width_rows, H, HD)
    value_rows = lax.dynamic_slice_in_dim(value_pad, query_start, 3 * width_rows, 0).reshape(3 * width_rows, H, HD)
    scores = jnp.einsum('thd,uhd->htu', query_rows, key_rows, precision=highest) * HD ** (-0.5)
    scores = low_back(scores)
    permit = allowed(query_start, width_rows, starts)
    scores = jnp.where(permit[None], scores, masked_score)
    attention = low(jax.nn.softmax(scores, axis=-1))
    mixed_rows = jnp.einsum('htu,uhd->thd', attention, value_rows, precision=highest)
    return mixed_rows.reshape(width_rows, D)

def block_layer(values, weights, starts):
    first_gain, first_shift, qkv_weight, query_bias, value_bias, out_weight, out_bias, second_gain, second_shift, up_weight, up_bias, down_weight, down_bias = weights
    first_in = low(norm_rows(values, first_gain, first_shift))
    joined = matmul(first_in, qkv_weight)
    queries = low_back(low(joined[:, :D] + query_bias))
    keys_all = low_back(low(joined[:, D:2 * D]))
    values_all = low_back(low(joined[:, 2 * D:] + value_bias))
    padding = ((MB_TOK, MB_TOK), (0, 0))
    key_pad = jnp.pad(keys_all, padding)
    value_pad = jnp.pad(values_all, padding)
    attend = jax.checkpoint(attend_block)

    def per_block(block_index):
        return attend(block_index, queries, key_pad, value_pad, starts)
    mixed_rows = lax.map(per_block, jnp.arange(N_FSDP, dtype=jnp.int32))
    mixed_rows = low_back(low(mixed_rows.reshape(N_FSDP * MB_TOK, D)))
    middle = values + low_back(matmul(mixed_rows, out_weight) + out_bias)
    second_in = low(norm_rows(middle, second_gain, second_shift))
    hidden = low_back(matmul(second_in, up_weight) + up_bias)
    active = low(jax.nn.gelu(hidden, approximate=False))
    return middle + matmul(active, down_weight) + down_bias

def reference(tokens, out_grad, image_starts, first_gain, first_shift, qkv_weight, query_bias, value_bias, out_weight, out_bias, second_gain, second_shift, up_weight, up_bias, down_weight, down_bias):
    weights = tuple((weight_arg.astype(jnp.float32) for weight_arg in (first_gain, first_shift, qkv_weight, query_bias, value_bias, out_weight, out_bias, second_gain, second_shift, up_weight, up_bias, down_weight, down_bias)))
    packed = N_FSDP * MB_TOK
    inputs = tokens.astype(jnp.float32).reshape(MICRO * N_REP, packed, D)
    cotangents = out_grad.astype(jnp.float32).reshape(MICRO * N_REP, packed, D)
    starts_all = image_starts.reshape(MICRO * N_REP, IMGS)

    def one_group(totals, slices):
        group_in, group_cot, group_starts = slices

        def apply_layer(values, params):
            return block_layer(values, params, group_starts)
        result, pullback = jax.vjp(apply_layer, group_in, weights)
        input_grad, weight_grads = pullback(group_cot)
        totals = jax.tree.map(jnp.add, totals, weight_grads)
        return (totals, (result.astype(jnp.bfloat16), input_grad.astype(jnp.bfloat16)))
    zero_grads = jax.tree.map(jnp.zeros_like, weights)
    totals, (results, input_grads) = lax.scan(one_group, zero_grads, (inputs, cotangents, starts_all))
    return (results.reshape(MICRO, TOKENS, D), input_grads.reshape(MICRO, TOKENS, D), totals[0], totals[1], totals[2], totals[3], totals[4], totals[5], totals[6], totals[7], totals[8], totals[9], totals[10], totals[11], totals[12])
```

```python
import jax
import jax.numpy as jnp
from jax import lax
from jax.experimental import pallas as pl
from jax.experimental.pallas import tpu as pltpu
from jax.sharding import PartitionSpec as P

D = 1024
HD = 64
IMG = 577


epsilon = 1e-06
masked_score = -1e30


def product(left, right):
    return jnp.dot(left, right, preferred_element_type=jnp.float32)


def product_left(left, right):
    return lax.dot_general(
        left, right, (((0,), (0,)), ((), ())), preferred_element_type=jnp.float32
    )


def product_right(left, right):
    return lax.dot_general(
        left, right, (((1,), (1,)), ((), ())), preferred_element_type=jnp.float32
    )


def norm_stats(values):
    centre = values - jnp.mean(values, axis=-1, keepdims=True)
    spread = jnp.mean(centre * centre, axis=-1, keepdims=True)
    factor = lax.rsqrt(spread + epsilon)
    return (centre * factor, factor)


def norm_back(grad_normed, normed, factor):
    return factor * (
        grad_normed
        - jnp.mean(grad_normed, axis=-1, keepdims=True)
        - normed * jnp.mean(grad_normed * normed, axis=-1, keepdims=True)
    )


QT = 192
KT = 192
PAIR = 128


def stacked_pair(rows):
    low = lax.broadcasted_iota(jnp.int32, rows.shape, 1) < HD
    zero = jnp.zeros_like(rows)
    return jnp.concatenate([jnp.where(low, rows, zero), jnp.where(low, zero, rows)], axis=0)


def merged_pair(columns):
    rows = columns.T
    half = rows.shape[0] // 2
    low = lax.broadcasted_iota(jnp.int32, (half, PAIR), 1) < HD
    return jnp.where(low, rows[:half], rows[half:])


def contract(left, right, left_dim, right_dim):
    return lax.dot_general(
        left,
        right,
        (((left_dim,), (right_dim,)), ((), ())),
        preferred_element_type=jnp.float32,
    )


def load_window(parts, window):
    rows = parts[0].shape[0]
    for index, part in enumerate(parts):
        window[index * rows : (index + 1) * rows, :] = part[...]


def tile_scores(key_rows, query_stack, key_label, query_label):
    scores = contract(key_rows, query_stack, 1, 1)
    wide = jnp.concatenate([key_label] * (query_stack.shape[0] // PAIR), axis=1)
    return jnp.where(wide == query_label, scores, masked_score)


def attend_forward_kernel(
    bounds,
    query,
    key_low,
    key_own,
    key_high,
    value_low,
    value_own,
    value_high,
    key_labels,
    query_labels,
    mixed,
    log_totals,
    keys,
    values,
):
    load_window((key_low, key_own, key_high), keys)
    load_window((value_low, value_own, value_high), values)
    for tile in range(query.shape[0] // QT):
        rows = slice(tile * QT, (tile + 1) * QT)
        query_stack = stacked_pair(query[rows, :] * jnp.bfloat16(HD**-0.5))
        query_label = query_labels[tile]
        width = 2 * QT

        def step(index, carry):
            largest, total, gathered = carry
            place = pl.ds(pl.multiple_of(index * KT, KT), KT)
            scores = tile_scores(keys[place, :], query_stack, key_labels[place, :], query_label)
            raised_to = jnp.maximum(largest, jnp.max(scores, axis=0, keepdims=True))
            raised = jnp.exp(scores - raised_to)
            fade = jnp.exp(largest - raised_to)
            total = total * fade + jnp.sum(raised, axis=0, keepdims=True)
            gathered = gathered * fade + contract(
                values[place, :], raised.astype(jnp.bfloat16), 0, 0
            )
            return (raised_to, total, gathered)

        largest, total, gathered = lax.fori_loop(
            bounds[2 * tile],
            bounds[2 * tile + 1],
            step,
            (
                jnp.full((1, width), masked_score, jnp.float32),
                jnp.zeros((1, width), jnp.float32),
                jnp.zeros((PAIR, width), jnp.float32),
            ),
        )
        mixed[rows, :] = merged_pair(gathered / total).astype(jnp.bfloat16)
        log_totals[0, tile] = largest + jnp.log(total)


def attend_backward_kernel(
    bounds,
    query,
    key_low,
    key_own,
    key_high,
    value_low,
    value_own,
    value_high,
    key_labels,
    query_labels,
    mixed,
    log_totals,
    grad_mixed,
    grad_query,
    grad_low,
    grad_own,
    grad_high,
    keys,
    values,
    grad_keys,
    grad_values,
):
    load_window((key_low, key_own, key_high), keys)
    load_window((value_low, value_own, value_high), values)
    grad_keys[...] = jnp.zeros_like(grad_keys)
    grad_values[...] = jnp.zeros_like(grad_values)
    for tile in range(query.shape[0] // QT):
        rows = slice(tile * QT, (tile + 1) * QT)
        query_stack = stacked_pair(query[rows, :] * jnp.bfloat16(HD**-0.5))
        grad_rows = grad_mixed[rows, :]
        grad_stack = stacked_pair(grad_rows)
        inner = grad_rows.astype(jnp.float32) * mixed[rows, :].astype(jnp.float32)
        row_inner = jnp.sum(stacked_pair(inner).T, axis=0, keepdims=True)
        query_label = query_labels[tile]
        log_total = log_totals[0, tile]

        def step(index, grad_columns):
            place = pl.ds(pl.multiple_of(index * KT, KT), KT)
            key_rows = keys[place, :]
            scores = tile_scores(key_rows, query_stack, key_labels[place, :], query_label)
            attention = jnp.exp(scores - log_total)
            grad_probs = contract(values[place, :], grad_stack, 1, 1)
            grad_scores = (attention * (grad_probs - row_inner)).astype(jnp.bfloat16)
            grad_keys[place, :] += contract(grad_scores, query_stack, 1, 0)
            grad_values[place, :] += contract(attention.astype(jnp.bfloat16), grad_stack, 1, 0)
            return grad_columns + contract(key_rows, grad_scores, 0, 0)

        grad_columns = lax.fori_loop(
            bounds[2 * tile],
            bounds[2 * tile + 1],
            step,
            jnp.zeros((PAIR, 2 * QT), jnp.float32),
        )
        grad_query[rows, :] = (merged_pair(grad_columns) * HD**-0.5).astype(jnp.bfloat16)
    shard_rows = query.shape[0]
    for slot, source in ((0, grad_keys), (1, grad_values)):
        grad_low[slot] = source[:shard_rows, :].astype(jnp.bfloat16)
        grad_own[slot] = source[shard_rows : 2 * shard_rows, :]
        grad_high[slot] = source[2 * shard_rows :, :].astype(jnp.bfloat16)


def attend_specs(shard_rows):
    tiles = shard_rows // QT
    column = pl.BlockSpec((shard_rows, PAIR), lambda pair, bounds: (0, pair))
    value = pl.BlockSpec((shard_rows, PAIR), lambda pair, bounds: (0, D // PAIR + pair))
    both = pl.BlockSpec((2, shard_rows, PAIR), lambda pair, bounds: (0, 0, pair))
    key_label = pl.BlockSpec((3 * shard_rows, PAIR), lambda pair, bounds: (0, 0))
    query_label = pl.BlockSpec((tiles, 1, 2 * QT), lambda pair, bounds: (0, 0, 0))
    log_total = pl.BlockSpec((1, tiles, 1, 2 * QT), lambda pair, bounds: (pair, 0, 0, 0))
    operands = [column] * 4 + [value] * 3 + [key_label, query_label]
    return column, both, log_total, operands


def attend_forward(bounds, query, low, own, high, key_labels, query_labels):
    shard_rows = query.shape[0]
    tiles = shard_rows // QT
    pairs = D // PAIR
    column, both, log_total, operands = attend_specs(shard_rows)
    window = pltpu.VMEM((3 * shard_rows, PAIR), jnp.bfloat16)
    pairs_seen = 2 * D * shard_rows * IMG * 2
    return pl.pallas_call(
        attend_forward_kernel,
        grid_spec=pltpu.PrefetchScalarGridSpec(
            num_scalar_prefetch=1,
            grid=(pairs,),
            in_specs=operands,
            out_specs=[column, log_total],
            scratch_shapes=[window, window],
        ),
        out_shape=[
            jax.ShapeDtypeStruct((shard_rows, D), jnp.bfloat16),
            jax.ShapeDtypeStruct((pairs, tiles, 1, 2 * QT), jnp.float32),
        ],
        cost_estimate=pl.CostEstimate(
            flops=4 * pairs_seen, bytes_accessed=20 * shard_rows * D, transcendentals=0
        ),
    )(bounds, query, low, own, high, low, own, high, key_labels, query_labels)


def attend_backward(
    bounds, query, low, own, high, key_labels, query_labels, mixed, log_totals, grad_mixed
):
    shard_rows = query.shape[0]
    column, both, log_total, operands = attend_specs(shard_rows)
    window = pltpu.VMEM((3 * shard_rows, PAIR), jnp.bfloat16)
    wide = pltpu.VMEM((3 * shard_rows, PAIR), jnp.float32)
    pairs_seen = 2 * D * shard_rows * IMG * 2
    rim = jax.ShapeDtypeStruct((2, shard_rows, D), jnp.bfloat16)
    return pl.pallas_call(
        attend_backward_kernel,
        grid_spec=pltpu.PrefetchScalarGridSpec(
            num_scalar_prefetch=1,
            grid=(D // PAIR,),
            in_specs=operands + [column, log_total, column],
            out_specs=[column, both, both, both],
            scratch_shapes=[window, window, wide, wide],
        ),
        out_shape=[
            jax.ShapeDtypeStruct((shard_rows, D), jnp.bfloat16),
            rim,
            jax.ShapeDtypeStruct((2, shard_rows, D), jnp.float32),
            rim,
        ],
        cost_estimate=pl.CostEstimate(
            flops=8 * pairs_seen, bytes_accessed=40 * shard_rows * D, transcendentals=0
        ),
    )(
        bounds,
        query,
        low,
        own,
        high,
        low,
        own,
        high,
        key_labels,
        query_labels,
        mixed,
        log_totals,
        grad_mixed,
    )


def attend_plan(query_start, shard_rows, starts):
    places = query_start - shard_rows + jnp.arange(3 * shard_rows, dtype=jnp.int32)
    after = starts[None, :] <= places[:, None]
    inside = after & (places[:, None] < starts[None, :] + IMG)
    counted = jnp.sum(after.astype(jnp.int32), axis=1) - 1
    owned = jnp.any(inside, axis=1)
    labels = jnp.where(owned, counted, -(2**24) - places)
    image = jnp.sum(jnp.where(inside, starts[None, :], 0), axis=1)
    own = slice(shard_rows, 2 * shard_rows)
    base = query_start - shard_rows
    first = jnp.where(owned, image, places)[own].reshape(-1, QT)[:, 0] - base
    last = jnp.where(owned, image + IMG, places + 1)[own].reshape(-1, QT)[:, -1] - base
    low = jnp.maximum(first, 0) // KT
    high = jnp.minimum((last + KT - 1) // KT, 3 * shard_rows // KT)
    bounds = jnp.stack([low, high], axis=1).reshape(-1).astype(jnp.int32)
    key_labels = jnp.broadcast_to(labels[:, None], (3 * shard_rows, PAIR))
    tiles = labels[own].reshape(-1, 1, QT)
    return bounds, key_labels, jnp.concatenate([tiles, tiles], axis=2)


def neighbours(low_going, high_going):
    count = lax.axis_size("fsdp")
    forward = [(i, i + 1) for i in range(count - 1)]
    backward = [(target, source) for source, target in forward]
    from_low = lax.ppermute(high_going, "fsdp", forward)
    from_high = lax.ppermute(low_going, "fsdp", backward)
    return from_low, from_high


def body(
    tokens,
    out_grad,
    image_starts,
    first_gain,
    first_shift,
    qkv_weight,
    query_bias,
    value_bias,
    out_weight,
    out_bias,
    second_gain,
    second_shift,
    up_weight,
    up_bias,
    down_weight,
    down_bias,
):
    micro_count, shard_rows, _ = tokens.shape
    query_start = lax.axis_index("fsdp") * shard_rows

    def gathered(shard):
        return lax.all_gather(shard, "fsdp", axis=0, tiled=True)

    small = jnp.concatenate(
        [
            jnp.stack(
                [
                    first_gain,
                    first_shift,
                    query_bias,
                    value_bias,
                    out_bias,
                    second_gain,
                    second_shift,
                    down_bias,
                ]
            ).reshape(-1),
            up_bias,
        ]
    )
    count = lax.axis_size("fsdp")
    small = gathered(small).reshape(count, -1).astype(jnp.float32)
    part = D // count
    (
        first_gain,
        first_shift,
        query_bias,
        value_bias,
        out_bias,
        second_gain,
        second_shift,
        down_bias,
    ) = [small[:, i * part : (i + 1) * part].reshape(-1) for i in range(8)]
    up_bias = small[:, 8 * part :].reshape(-1)
    qkv_weight = gathered(qkv_weight)
    out_weight = gathered(out_weight)
    up_weight = gathered(up_weight)
    down_weight = gathered(down_weight)

    plans = [
        attend_plan(query_start, shard_rows, image_starts[micro, 0])
        for micro in range(micro_count)
    ]
    inputs = tokens.reshape(-1, D).astype(jnp.float32)
    normed_one, factor_one = norm_stats(inputs)
    first_in = (normed_one * first_gain + first_shift).astype(jnp.bfloat16)
    joined_bias = jnp.concatenate([query_bias, jnp.zeros_like(query_bias), value_bias])
    joined = (product(first_in, qkv_weight) + joined_bias).astype(jnp.bfloat16)
    operands = []
    mixed_parts = []
    for micro in range(micro_count):
        rows = joined[micro * shard_rows : (micro + 1) * shard_rows]
        own = rows[:, D:]
        low, high = neighbours(own, own)
        bounds, key_labels, query_labels = plans[micro]
        operand = (bounds, rows[:, :D], low, own, high, key_labels, query_labels)
        mixed, log_totals = attend_forward(*operand)
        operands.append(operand + (mixed, log_totals))
        mixed_parts.append(mixed)
    mixed_rows = jnp.concatenate(mixed_parts, axis=0)
    middle = inputs + product(mixed_rows, out_weight) + out_bias
    normed_two, factor_two = norm_stats(middle)
    second_in = (normed_two * second_gain + second_shift).astype(jnp.bfloat16)
    hidden = product(second_in, up_weight) + up_bias
    phi = 0.5 * (1.0 + lax.erf(hidden * (2.0**-0.5)))
    active = (hidden * phi).astype(jnp.bfloat16)
    slope = phi + hidden * jnp.exp(-0.5 * hidden * hidden) * ((2.0 * jnp.pi) ** -0.5)
    layer_out = (middle + product(active, down_weight) + down_bias).astype(jnp.bfloat16)

    cotangent = out_grad.reshape(-1, D)
    grad_out = cotangent.astype(jnp.float32)
    down_grad = product_left(active, cotangent)
    down_bias_grad = jnp.sum(grad_out, axis=0)
    grad_hidden = (product_right(cotangent, down_weight) * slope).astype(jnp.bfloat16)
    up_grad = product_left(second_in, grad_hidden)
    up_bias_grad = jnp.sum(grad_hidden.astype(jnp.float32), axis=0)
    grad_second = product_right(grad_hidden, up_weight)
    second_gain_grad = jnp.sum(grad_second * normed_two, axis=0)
    second_shift_grad = jnp.sum(grad_second, axis=0)
    grad_middle = grad_out + norm_back(grad_second * second_gain, normed_two, factor_two)
    grad_branch = grad_middle.astype(jnp.bfloat16)
    out_weight_grad = product_left(mixed_rows, grad_branch)
    out_bias_grad = jnp.sum(grad_branch.astype(jnp.float32), axis=0)
    grad_mixed = product_right(grad_branch, out_weight).astype(jnp.bfloat16)
    grad_queries = []
    grad_pairs = []
    for micro in range(micro_count):
        grad_query, grad_low, grad_own, grad_high = attend_backward(
            *operands[micro], grad_mixed[micro * shard_rows : (micro + 1) * shard_rows]
        )
        from_low, from_high = neighbours(grad_low, grad_high)
        grad_pair = (
            grad_own + from_low.astype(jnp.float32) + from_high.astype(jnp.float32)
        ).astype(jnp.bfloat16)
        grad_queries.append(grad_query)
        grad_pairs.append(grad_pair)
    grad_joined = jnp.concatenate(
        [
            jnp.concatenate([query_part, pair[0], pair[1]], axis=1)
            for query_part, pair in zip(grad_queries, grad_pairs)
        ],
        axis=0,
    )
    qkv_grad = product_left(first_in, grad_joined)
    joined_sums = jnp.sum(grad_joined.astype(jnp.float32), axis=0)
    grad_first = product_right(grad_joined, qkv_weight)
    first_gain_grad = jnp.sum(grad_first * normed_one, axis=0)
    first_shift_grad = jnp.sum(grad_first, axis=0)
    tokens_grad = (
        grad_middle + norm_back(grad_first * first_gain, normed_one, factor_one)
    ).astype(jnp.bfloat16)

    def reduced(grad):
        return lax.psum_scatter(
            grad.astype(jnp.bfloat16), "fsdp", scatter_dimension=0, tiled=True
        )

    def replicas(grad):
        return lax.psum(grad, "rep").astype(jnp.float32)

    small_grads = [
        first_gain_grad,
        first_shift_grad,
        joined_sums[:D],
        joined_sums[2 * D :],
        out_bias_grad,
        second_gain_grad,
        second_shift_grad,
        down_bias_grad,
        up_bias_grad,
    ]
    packed = jnp.concatenate([grad.reshape(count, -1) for grad in small_grads], axis=1)
    packed = lax.psum(packed, ("rep", "fsdp"))
    packed = lax.dynamic_index_in_dim(packed, lax.axis_index("fsdp"), 0, keepdims=False)
    smalls = [packed[i * part : (i + 1) * part] for i in range(8)] + [packed[8 * part :]]
    down_grad = replicas(reduced(down_grad))
    up_grad = replicas(reduced(up_grad))
    out_weight_grad = replicas(reduced(out_weight_grad))
    qkv_grad = replicas(reduced(qkv_grad))
    return (
        layer_out.reshape(tokens.shape),
        tokens_grad.reshape(tokens.shape),
        smalls[0],
        smalls[1],
        qkv_grad,
        smalls[2],
        smalls[3],
        out_weight_grad,
        smalls[4],
        smalls[5],
        smalls[6],
        up_grad,
        smalls[8],
        down_grad,
        smalls[7],
    )


def solution(mesh):
    placed = (
        P(None, ("rep", "fsdp"), None),
        P(None, ("rep", "fsdp"), None),
        P(None, "rep", None),
        P("fsdp"),
        P("fsdp"),
        P("fsdp", None),
        P("fsdp"),
        P("fsdp"),
        P("fsdp", None),
        P("fsdp"),
        P("fsdp"),
        P("fsdp"),
        P("fsdp", None),
        P("fsdp"),
        P("fsdp", None),
        P("fsdp"),
    )
    return jax.shard_map(
        body,
        mesh=mesh,
        in_specs=placed,
        out_specs=(
            P(None, ("rep", "fsdp"), None),
            P(None, ("rep", "fsdp"), None),
            P("fsdp"),
            P("fsdp"),
            P("fsdp", None),
            P("fsdp"),
            P("fsdp"),
            P("fsdp", None),
            P("fsdp"),
            P("fsdp"),
            P("fsdp"),
            P("fsdp", None),
            P("fsdp"),
            P("fsdp", None),
            P("fsdp"),
        ),
        check_vma=False,
    )
```

```python
import jax
import jax.numpy as jnp
from jax import lax
from jax.experimental import pallas as pl
from jax.experimental.pallas import tpu as pltpu
from jax.sharding import PartitionSpec as P

D = 1024
HD = 64
IMG = 577


epsilon = 1e-06
masked_score = -1e30


def product(left, right):
    return jnp.dot(left, right, preferred_element_type=jnp.float32)


def product_left(left, right):
    return lax.dot_general(
        left, right, (((0,), (0,)), ((), ())), preferred_element_type=jnp.float32
    )


def product_right(left, right):
    return lax.dot_general(
        left, right, (((1,), (1,)), ((), ())), preferred_element_type=jnp.float32
    )


def norm_stats(values):
    centre = values - jnp.mean(values, axis=-1, keepdims=True)
    spread = jnp.mean(centre * centre, axis=-1, keepdims=True)
    factor = lax.rsqrt(spread + epsilon)
    return (centre * factor, factor)


def norm_back(grad_normed, normed, factor):
    return factor * (
        grad_normed
        - jnp.mean(grad_normed, axis=-1, keepdims=True)
        - normed * jnp.mean(grad_normed * normed, axis=-1, keepdims=True)
    )


QT = 192
KT = 192
PAIR = 128


def stacked_pair(rows):
    low = lax.broadcasted_iota(jnp.int32, rows.shape, 1) < HD
    zero = jnp.zeros_like(rows)
    return jnp.concatenate([jnp.where(low, rows, zero), jnp.where(low, zero, rows)], axis=0)


def merged_pair(columns):
    rows = columns.T
    half = rows.shape[0] // 2
    low = lax.broadcasted_iota(jnp.int32, (half, PAIR), 1) < HD
    return jnp.where(low, rows[:half], rows[half:])


def contract(left, right, left_dim, right_dim):
    return lax.dot_general(
        left,
        right,
        (((left_dim,), (right_dim,)), ((), ())),
        preferred_element_type=jnp.float32,
    )


def load_window(parts, window):
    rows = parts[0].shape[0]
    for index, part in enumerate(parts):
        window[index * rows : (index + 1) * rows, :] = part[...]


def tile_scores(key_rows, query_stack, key_label, query_label):
    scores = contract(key_rows, query_stack, 1, 1)
    wide = jnp.concatenate([key_label] * (query_stack.shape[0] // PAIR), axis=1)
    return jnp.where(wide == query_label, scores, masked_score)


def attend_forward_kernel(
    bounds,
    query,
    key_low,
    key_own,
    key_high,
    value_low,
    value_own,
    value_high,
    key_labels,
    query_labels,
    mixed,
    log_totals,
    keys,
    values,
):
    load_window((key_low, key_own, key_high), keys)
    load_window((value_low, value_own, value_high), values)
    for tile in range(query.shape[0] // QT):
        rows = slice(tile * QT, (tile + 1) * QT)
        query_stack = stacked_pair(query[rows, :] * jnp.bfloat16(HD**-0.5))
        query_label = query_labels[tile]
        width = 2 * QT

        def step(index, carry):
            largest, total, gathered = carry
            place = pl.ds(pl.multiple_of(index * KT, KT), KT)
            scores = tile_scores(keys[place, :], query_stack, key_labels[place, :], query_label)
            raised_to = jnp.maximum(largest, jnp.max(scores, axis=0, keepdims=True))
            raised = jnp.exp(scores - raised_to)
            fade = jnp.exp(largest - raised_to)
            total = total * fade + jnp.sum(raised, axis=0, keepdims=True)
            gathered = gathered * fade + contract(
                values[place, :], raised.astype(jnp.bfloat16), 0, 0
            )
            return (raised_to, total, gathered)

        largest, total, gathered = lax.fori_loop(
            bounds[2 * tile],
            bounds[2 * tile + 1],
            step,
            (
                jnp.full((1, width), masked_score, jnp.float32),
                jnp.zeros((1, width), jnp.float32),
                jnp.zeros((PAIR, width), jnp.float32),
            ),
        )
        mixed[rows, :] = merged_pair(gathered / total).astype(jnp.bfloat16)
        log_totals[0, tile] = largest + jnp.log(total)


def attend_backward_kernel(
    bounds,
    query,
    key_low,
    key_own,
    key_high,
    value_low,
    value_own,
    value_high,
    key_labels,
    query_labels,
    mixed,
    log_totals,
    grad_mixed,
    grad_query,
    grad_low,
    grad_own,
    grad_high,
    keys,
    values,
    grad_keys,
    grad_values,
):
    load_window((key_low, key_own, key_high), keys)
    load_window((value_low, value_own, value_high), values)
    grad_keys[...] = jnp.zeros_like(grad_keys)
    grad_values[...] = jnp.zeros_like(grad_values)
    for tile in range(query.shape[0] // QT):
        rows = slice(tile * QT, (tile + 1) * QT)
        query_stack = stacked_pair(query[rows, :] * jnp.bfloat16(HD**-0.5))
        grad_rows = grad_mixed[rows, :]
        grad_stack = stacked_pair(grad_rows)
        inner = grad_rows.astype(jnp.float32) * mixed[rows, :].astype(jnp.float32)
        row_inner = jnp.sum(stacked_pair(inner).T, axis=0, keepdims=True)
        query_label = query_labels[tile]
        log_total = log_totals[0, tile]

        def step(index, grad_columns):
            place = pl.ds(pl.multiple_of(index * KT, KT), KT)
            key_rows = keys[place, :]
            scores = tile_scores(key_rows, query_stack, key_labels[place, :], query_label)
            attention = jnp.exp(scores - log_total)
            grad_probs = contract(values[place, :], grad_stack, 1, 1)
            grad_scores = (attention * (grad_probs - row_inner)).astype(jnp.bfloat16)
            grad_keys[place, :] += contract(grad_scores, query_stack, 1, 0)
            grad_values[place, :] += contract(attention.astype(jnp.bfloat16), grad_stack, 1, 0)
            return grad_columns + contract(key_rows, grad_scores, 0, 0)

        grad_columns = lax.fori_loop(
            bounds[2 * tile],
            bounds[2 * tile + 1],
            step,
            jnp.zeros((PAIR, 2 * QT), jnp.float32),
        )
        grad_query[rows, :] = (merged_pair(grad_columns) * HD**-0.5).astype(jnp.bfloat16)
    shard_rows = query.shape[0]
    for slot, source in ((0, grad_keys), (1, grad_values)):
        grad_low[slot] = source[:shard_rows, :].astype(jnp.bfloat16)
        grad_own[slot] = source[shard_rows : 2 * shard_rows, :]
        grad_high[slot] = source[2 * shard_rows :, :].astype(jnp.bfloat16)


def attend_specs(shard_rows):
    tiles = shard_rows // QT
    column = pl.BlockSpec((shard_rows, PAIR), lambda pair, bounds: (0, pair))
    value = pl.BlockSpec((shard_rows, PAIR), lambda pair, bounds: (0, D // PAIR + pair))
    both = pl.BlockSpec((2, shard_rows, PAIR), lambda pair, bounds: (0, 0, pair))
    key_label = pl.BlockSpec((3 * shard_rows, PAIR), lambda pair, bounds: (0, 0))
    query_label = pl.BlockSpec((tiles, 1, 2 * QT), lambda pair, bounds: (0, 0, 0))
    log_total = pl.BlockSpec((1, tiles, 1, 2 * QT), lambda pair, bounds: (pair, 0, 0, 0))
    operands = [column] * 4 + [value] * 3 + [key_label, query_label]
    return column, both, log_total, operands


def attend_forward(bounds, query, low, own, high, key_labels, query_labels):
    shard_rows = query.shape[0]
    tiles = shard_rows // QT
    pairs = D // PAIR
    column, both, log_total, operands = attend_specs(shard_rows)
    window = pltpu.VMEM((3 * shard_rows, PAIR), jnp.bfloat16)
    pairs_seen = 2 * D * shard_rows * IMG * 2
    return pl.pallas_call(
        attend_forward_kernel,
        grid_spec=pltpu.PrefetchScalarGridSpec(
            num_scalar_prefetch=1,
            grid=(pairs,),
            in_specs=operands,
            out_specs=[column, log_total],
            scratch_shapes=[window, window],
        ),
        out_shape=[
            jax.ShapeDtypeStruct((shard_rows, D), jnp.bfloat16),
            jax.ShapeDtypeStruct((pairs, tiles, 1, 2 * QT), jnp.float32),
        ],
        cost_estimate=pl.CostEstimate(
            flops=4 * pairs_seen, bytes_accessed=20 * shard_rows * D, transcendentals=0
        ),
    )(bounds, query, low, own, high, low, own, high, key_labels, query_labels)


def attend_backward(
    bounds, query, low, own, high, key_labels, query_labels, mixed, log_totals, grad_mixed
):
    shard_rows = query.shape[0]
    column, both, log_total, operands = attend_specs(shard_rows)
    window = pltpu.VMEM((3 * shard_rows, PAIR), jnp.bfloat16)
    wide = pltpu.VMEM((3 * shard_rows, PAIR), jnp.float32)
    pairs_seen = 2 * D * shard_rows * IMG * 2
    rim = jax.ShapeDtypeStruct((2, shard_rows, D), jnp.bfloat16)
    return pl.pallas_call(
        attend_backward_kernel,
        grid_spec=pltpu.PrefetchScalarGridSpec(
            num_scalar_prefetch=1,
            grid=(D // PAIR,),
            in_specs=operands + [column, log_total, column],
            out_specs=[column, both, both, both],
            scratch_shapes=[window, window, wide, wide],
        ),
        out_shape=[
            jax.ShapeDtypeStruct((shard_rows, D), jnp.bfloat16),
            rim,
            jax.ShapeDtypeStruct((2, shard_rows, D), jnp.float32),
            rim,
        ],
        cost_estimate=pl.CostEstimate(
            flops=8 * pairs_seen, bytes_accessed=40 * shard_rows * D, transcendentals=0
        ),
    )(
        bounds,
        query,
        low,
        own,
        high,
        low,
        own,
        high,
        key_labels,
        query_labels,
        mixed,
        log_totals,
        grad_mixed,
    )


def attend_plan(query_start, shard_rows, starts):
    places = query_start - shard_rows + jnp.arange(3 * shard_rows, dtype=jnp.int32)
    after = starts[None, :] <= places[:, None]
    inside = after & (places[:, None] < starts[None, :] + IMG)
    counted = jnp.sum(after.astype(jnp.int32), axis=1) - 1
    owned = jnp.any(inside, axis=1)
    labels = jnp.where(owned, counted, -(2**24) - places)
    image = jnp.sum(jnp.where(inside, starts[None, :], 0), axis=1)
    own = slice(shard_rows, 2 * shard_rows)
    base = query_start - shard_rows
    first = jnp.where(owned, image, places)[own].reshape(-1, QT)[:, 0] - base
    last = jnp.where(owned, image + IMG, places + 1)[own].reshape(-1, QT)[:, -1] - base
    low = jnp.maximum(first, 0) // KT
    high = jnp.minimum((last + KT - 1) // KT, 3 * shard_rows // KT)
    bounds = jnp.stack([low, high], axis=1).reshape(-1).astype(jnp.int32)
    key_labels = jnp.broadcast_to(labels[:, None], (3 * shard_rows, PAIR))
    tiles = labels[own].reshape(-1, 1, QT)
    return bounds, key_labels, jnp.concatenate([tiles, tiles], axis=2)


def neighbours(low_going, high_going):
    count = lax.axis_size("fsdp")
    forward = [(i, i + 1) for i in range(count - 1)]
    backward = [(target, source) for source, target in forward]
    from_low = lax.ppermute(high_going, "fsdp", forward)
    from_high = lax.ppermute(low_going, "fsdp", backward)
    return from_low, from_high


def swapped(value, axis, bit):
    count = lax.axis_size(axis)
    return lax.ppermute(value, axis, [(i, i ^ bit) for i in range(count)])


def picked(value, dim, half, bit):
    size = value.shape[dim] // 2
    return lax.dynamic_slice_in_dim(value, (bit ^ half) * size, size, axis=dim)


def halved(value, dim, axis, bit):
    mine = (lax.axis_index(axis) // bit) % 2
    arrived = swapped(picked(value, dim, 1, mine), axis, bit)
    return picked(value, dim, 0, mine) + arrived


def doubled(value, dim, axis, bit):
    mine = (lax.axis_index(axis) // bit) % 2
    arrived = swapped(value, axis, bit)
    low = jnp.where(mine == 0, value, arrived)
    high = jnp.where(mine == 0, arrived, value)
    return jnp.concatenate([low, high], axis=dim)


def over_fsdp(value):
    count = lax.axis_size("fsdp")
    outer = count // 2
    rows, columns = value.shape[1:]
    value = value.reshape(outer, 2 * rows, columns)
    value = halved(value, 1, "fsdp", 1)
    bit = 2
    span = outer
    value = value.reshape(span, rows, columns)
    while span > 1:
        value = value.reshape(span // 2, 2 * rows, columns)
        value = halved(value, 1, "fsdp", bit)
        span //= 2
        bit *= 2
    return value.reshape(rows, columns)


def reduce_all(grad):
    count = lax.axis_size("fsdp")
    value = grad.astype(jnp.bfloat16).reshape(count, -1, grad.shape[1])
    value = halved(value, 1, "rep", 1)
    half = value.shape[1] // 2
    first = halved(value[:, :half], 1, "rep", 2)
    first = over_fsdp(first)
    second = over_fsdp(value[:, half:])
    first = doubled(first, 0, "rep", 2)
    second = second + swapped(second, "rep", 2)
    return doubled(jnp.concatenate([first, second], axis=0), 0, "rep", 1).astype(jnp.float32)


def body(
    tokens,
    out_grad,
    image_starts,
    first_gain,
    first_shift,
    qkv_weight,
    query_bias,
    value_bias,
    out_weight,
    out_bias,
    second_gain,
    second_shift,
    up_weight,
    up_bias,
    down_weight,
    down_bias,
):
    micro_count, shard_rows, _ = tokens.shape
    query_start = lax.axis_index("fsdp") * shard_rows

    def gathered(shard):
        rows = shard.shape[0] // lax.axis_size("rep")
        mine = lax.dynamic_slice_in_dim(shard, lax.axis_index("rep") * rows, rows, axis=0)
        return lax.all_gather(mine, ("fsdp", "rep"), axis=0, tiled=True)

    small = jnp.concatenate(
        [
            jnp.stack(
                [
                    first_gain,
                    first_shift,
                    query_bias,
                    value_bias,
                    out_bias,
                    second_gain,
                    second_shift,
                    down_bias,
                ]
            ).reshape(-1),
            up_bias,
        ]
    )
    count = lax.axis_size("fsdp")
    small = gathered(small).reshape(count, -1).astype(jnp.float32)
    part = D // count
    (
        first_gain,
        first_shift,
        query_bias,
        value_bias,
        out_bias,
        second_gain,
        second_shift,
        down_bias,
    ) = [small[:, i * part : (i + 1) * part].reshape(-1) for i in range(8)]
    up_bias = small[:, 8 * part :].reshape(-1)
    qkv_weight = gathered(qkv_weight)
    out_weight = gathered(out_weight)
    up_weight = gathered(up_weight)
    down_weight = gathered(down_weight)

    plans = [
        attend_plan(query_start, shard_rows, image_starts[micro, 0])
        for micro in range(micro_count)
    ]
    inputs = tokens.reshape(-1, D).astype(jnp.float32)
    normed_one, factor_one = norm_stats(inputs)
    first_in = (normed_one * first_gain + first_shift).astype(jnp.bfloat16)
    joined_bias = jnp.concatenate([query_bias, jnp.zeros_like(query_bias), value_bias])
    joined = (product(first_in, qkv_weight) + joined_bias).astype(jnp.bfloat16)
    operands = []
    mixed_parts = []
    for micro in range(micro_count):
        rows = joined[micro * shard_rows : (micro + 1) * shard_rows]
        own = rows[:, D:]
        low, high = neighbours(own, own)
        bounds, key_labels, query_labels = plans[micro]
        operand = (bounds, rows[:, :D], low, own, high, key_labels, query_labels)
        mixed, log_totals = attend_forward(*operand)
        operands.append(operand + (mixed, log_totals))
        mixed_parts.append(mixed)
    mixed_rows = jnp.concatenate(mixed_parts, axis=0)
    middle = inputs + product(mixed_rows, out_weight) + out_bias
    normed_two, factor_two = norm_stats(middle)
    second_in = (normed_two * second_gain + second_shift).astype(jnp.bfloat16)
    hidden = product(second_in, up_weight) + up_bias
    phi = 0.5 * (1.0 + lax.erf(hidden * (2.0**-0.5)))
    active = (hidden * phi).astype(jnp.bfloat16)
    slope = phi + hidden * jnp.exp(-0.5 * hidden * hidden) * ((2.0 * jnp.pi) ** -0.5)
    layer_out = (middle + product(active, down_weight) + down_bias).astype(jnp.bfloat16)

    cotangent = out_grad.reshape(-1, D)
    grad_out = cotangent.astype(jnp.float32)
    down_grad = product_left(active, cotangent)
    down_bias_grad = jnp.sum(grad_out, axis=0)
    grad_hidden = (product_right(cotangent, down_weight) * slope).astype(jnp.bfloat16)
    up_grad = product_left(second_in, grad_hidden)
    up_bias_grad = jnp.sum(grad_hidden.astype(jnp.float32), axis=0)
    grad_second = product_right(grad_hidden, up_weight)
    second_gain_grad = jnp.sum(grad_second * normed_two, axis=0)
    second_shift_grad = jnp.sum(grad_second, axis=0)
    grad_middle = grad_out + norm_back(grad_second * second_gain, normed_two, factor_two)
    grad_branch = grad_middle.astype(jnp.bfloat16)
    out_weight_grad = product_left(mixed_rows, grad_branch)
    out_bias_grad = jnp.sum(grad_branch.astype(jnp.float32), axis=0)
    grad_mixed = product_right(grad_branch, out_weight).astype(jnp.bfloat16)
    grad_queries = []
    grad_pairs = []
    for micro in range(micro_count):
        grad_query, grad_low, grad_own, grad_high = attend_backward(
            *operands[micro], grad_mixed[micro * shard_rows : (micro + 1) * shard_rows]
        )
        from_low, from_high = neighbours(grad_low, grad_high)
        grad_pair = (
            grad_own + from_low.astype(jnp.float32) + from_high.astype(jnp.float32)
        ).astype(jnp.bfloat16)
        grad_queries.append(grad_query)
        grad_pairs.append(grad_pair)
    grad_joined = jnp.concatenate(
        [
            jnp.concatenate([query_part, pair[0], pair[1]], axis=1)
            for query_part, pair in zip(grad_queries, grad_pairs)
        ],
        axis=0,
    )
    qkv_grad = product_left(first_in, grad_joined)
    joined_sums = jnp.sum(grad_joined.astype(jnp.float32), axis=0)
    grad_first = product_right(grad_joined, qkv_weight)
    first_gain_grad = jnp.sum(grad_first * normed_one, axis=0)
    first_shift_grad = jnp.sum(grad_first, axis=0)
    tokens_grad = (
        grad_middle + norm_back(grad_first * first_gain, normed_one, factor_one)
    ).astype(jnp.bfloat16)

    small_grads = [
        first_gain_grad,
        first_shift_grad,
        joined_sums[:D],
        joined_sums[2 * D :],
        out_bias_grad,
        second_gain_grad,
        second_shift_grad,
        down_bias_grad,
        up_bias_grad,
    ]
    packed = jnp.concatenate([grad.reshape(count, -1) for grad in small_grads], axis=1)
    width = packed.shape[1]
    lanes = -(-width // 2048) * 128
    packed = jnp.pad(packed, ((0, 0), (0, 16 * lanes - width)))
    packed = reduce_all(packed.reshape(count * 16, lanes)).reshape(-1)
    smalls = [packed[i * part : (i + 1) * part] for i in range(8)] + [packed[8 * part : width]]
    down_grad = reduce_all(down_grad)
    up_grad = reduce_all(up_grad)
    out_weight_grad = reduce_all(out_weight_grad)
    qkv_grad = reduce_all(qkv_grad)
    return (
        layer_out.reshape(tokens.shape),
        tokens_grad.reshape(tokens.shape),
        smalls[0],
        smalls[1],
        qkv_grad,
        smalls[2],
        smalls[3],
        out_weight_grad,
        smalls[4],
        smalls[5],
        smalls[6],
        up_grad,
        smalls[8],
        down_grad,
        smalls[7],
    )


def solution(mesh):
    placed = (
        P(None, ("rep", "fsdp"), None),
        P(None, ("rep", "fsdp"), None),
        P(None, "rep", None),
        P("fsdp"),
        P("fsdp"),
        P("fsdp", None),
        P("fsdp"),
        P("fsdp"),
        P("fsdp", None),
        P("fsdp"),
        P("fsdp"),
        P("fsdp"),
        P("fsdp", None),
        P("fsdp"),
        P("fsdp", None),
        P("fsdp"),
    )
    return jax.shard_map(
        body,
        mesh=mesh,
        in_specs=placed,
        out_specs=(
            P(None, ("rep", "fsdp"), None),
            P(None, ("rep", "fsdp"), None),
            P("fsdp"),
            P("fsdp"),
            P("fsdp", None),
            P("fsdp"),
            P("fsdp"),
            P("fsdp", None),
            P("fsdp"),
            P("fsdp"),
            P("fsdp"),
            P("fsdp", None),
            P("fsdp"),
            P("fsdp", None),
            P("fsdp"),
        ),
        check_vma=False,
    )
```

```python
import jax
import jax.numpy as jnp
from jax import lax
from jax.experimental import pallas as pl
from jax.experimental.pallas import tpu as pltpu
from jax.sharding import PartitionSpec as P

D = 1024
HD = 64
IMG = 577


epsilon = 1e-06
masked_score = -1e30


def product(left, right):
    return jnp.dot(left, right, preferred_element_type=jnp.float32)


def product_left(left, right):
    return lax.dot_general(
        left, right, (((0,), (0,)), ((), ())), preferred_element_type=jnp.float32
    )


def product_right(left, right):
    return lax.dot_general(
        left, right, (((1,), (1,)), ((), ())), preferred_element_type=jnp.float32
    )


def norm_stats(values):
    centre = values - jnp.mean(values, axis=-1, keepdims=True)
    spread = jnp.mean(centre * centre, axis=-1, keepdims=True)
    factor = lax.rsqrt(spread + epsilon)
    return (centre * factor, factor)


def norm_back(grad_normed, normed, factor):
    return factor * (
        grad_normed
        - jnp.mean(grad_normed, axis=-1, keepdims=True)
        - normed * jnp.mean(grad_normed * normed, axis=-1, keepdims=True)
    )


QT = 192
KT = 192
PAIR = 128


def stacked_pair(rows):
    low = lax.broadcasted_iota(jnp.int32, rows.shape, 1) < HD
    zero = jnp.zeros_like(rows)
    return jnp.concatenate([jnp.where(low, rows, zero), jnp.where(low, zero, rows)], axis=0)


def merged_pair(columns):
    rows = columns.T
    half = rows.shape[0] // 2
    low = lax.broadcasted_iota(jnp.int32, (half, PAIR), 1) < HD
    return jnp.where(low, rows[:half], rows[half:])


def contract(left, right, left_dim, right_dim):
    return lax.dot_general(
        left,
        right,
        (((left_dim,), (right_dim,)), ((), ())),
        preferred_element_type=jnp.float32,
    )


def load_window(parts, window):
    rows = parts[0].shape[0]
    for index, part in enumerate(parts):
        window[index * rows : (index + 1) * rows, :] = part[...]


def tile_scores(key_rows, query_stack, key_label, query_label):
    scores = contract(key_rows, query_stack, 1, 1)
    wide = jnp.concatenate([key_label] * (query_stack.shape[0] // PAIR), axis=1)
    return jnp.where(wide == query_label, scores, masked_score)


def attend_forward_kernel(
    bounds,
    query,
    key_low,
    key_own,
    key_high,
    value_low,
    value_own,
    value_high,
    key_labels,
    query_labels,
    mixed,
    log_totals,
    keys,
    values,
):
    load_window((key_low, key_own, key_high), keys)
    load_window((value_low, value_own, value_high), values)
    for tile in range(query.shape[0] // QT):
        rows = slice(tile * QT, (tile + 1) * QT)
        query_stack = stacked_pair(query[rows, :] * jnp.bfloat16(HD**-0.5))
        query_label = query_labels[tile]
        width = 2 * QT

        def step(index, carry):
            largest, total, gathered = carry
            place = pl.ds(pl.multiple_of(index * KT, KT), KT)
            scores = tile_scores(keys[place, :], query_stack, key_labels[place, :], query_label)
            raised_to = jnp.maximum(largest, jnp.max(scores, axis=0, keepdims=True))
            raised = jnp.exp(scores - raised_to)
            fade = jnp.exp(largest - raised_to)
            total = total * fade + jnp.sum(raised, axis=0, keepdims=True)
            gathered = gathered * fade + contract(
                values[place, :], raised.astype(jnp.bfloat16), 0, 0
            )
            return (raised_to, total, gathered)

        largest, total, gathered = lax.fori_loop(
            bounds[2 * tile],
            bounds[2 * tile + 1],
            step,
            (
                jnp.full((1, width), masked_score, jnp.float32),
                jnp.zeros((1, width), jnp.float32),
                jnp.zeros((PAIR, width), jnp.float32),
            ),
        )
        mixed[rows, :] = merged_pair(gathered / total).astype(jnp.bfloat16)
        log_totals[0, tile] = largest + jnp.log(total)


def attend_backward_kernel(
    bounds,
    query,
    key_low,
    key_own,
    key_high,
    value_low,
    value_own,
    value_high,
    key_labels,
    query_labels,
    mixed,
    log_totals,
    grad_mixed,
    grad_query,
    grad_own,
    grad_rims,
    keys,
    values,
    grad_keys,
    grad_values,
):
    load_window((key_low, key_own, key_high), keys)
    load_window((value_low, value_own, value_high), values)
    grad_keys[...] = jnp.zeros_like(grad_keys)
    grad_values[...] = jnp.zeros_like(grad_values)
    for tile in range(query.shape[0] // QT):
        rows = slice(tile * QT, (tile + 1) * QT)
        query_stack = stacked_pair(query[rows, :] * jnp.bfloat16(HD**-0.5))
        grad_rows = grad_mixed[rows, :]
        grad_stack = stacked_pair(grad_rows)
        inner = grad_rows.astype(jnp.float32) * mixed[rows, :].astype(jnp.float32)
        row_inner = jnp.sum(stacked_pair(inner).T, axis=0, keepdims=True)
        query_label = query_labels[tile]
        log_total = log_totals[0, tile]

        def step(index, grad_columns):
            place = pl.ds(pl.multiple_of(index * KT, KT), KT)
            key_rows = keys[place, :]
            scores = tile_scores(key_rows, query_stack, key_labels[place, :], query_label)
            attention = jnp.exp(scores - log_total)
            grad_probs = contract(values[place, :], grad_stack, 1, 1)
            grad_scores = (attention * (grad_probs - row_inner)).astype(jnp.bfloat16)
            grad_keys[place, :] += contract(grad_scores, query_stack, 1, 0)
            grad_values[place, :] += contract(attention.astype(jnp.bfloat16), grad_stack, 1, 0)
            return grad_columns + contract(key_rows, grad_scores, 0, 0)

        grad_columns = lax.fori_loop(
            bounds[2 * tile],
            bounds[2 * tile + 1],
            step,
            jnp.zeros((PAIR, 2 * QT), jnp.float32),
        )
        grad_query[rows, :] = (merged_pair(grad_columns) * HD**-0.5).astype(jnp.bfloat16)
    shard_rows = query.shape[0]
    for slot, source in ((0, grad_keys), (1, grad_values)):
        grad_rims[slot, :shard_rows] = source[:shard_rows, :].astype(jnp.bfloat16)
        grad_own[slot] = source[shard_rows : 2 * shard_rows, :].astype(jnp.bfloat16)
        grad_rims[slot, shard_rows:] = source[2 * shard_rows :, :].astype(jnp.bfloat16)


def attend_specs(shard_rows):
    tiles = shard_rows // QT
    pairs = D // PAIR

    def block(row, column):
        return pl.BlockSpec((shard_rows, PAIR), lambda pair, bounds: (row, column + pair))

    column = block(0, 0)
    key_label = pl.BlockSpec((3 * shard_rows, PAIR), lambda pair, bounds: (0, 0))
    query_label = pl.BlockSpec((tiles, 1, 2 * QT), lambda pair, bounds: (0, 0, 0))
    log_total = pl.BlockSpec((1, tiles, 1, 2 * QT), lambda pair, bounds: (pair, 0, 0, 0))
    operands = [
        column,
        block(0, 0),
        block(0, pairs),
        block(1, 0),
        block(0, pairs),
        block(0, 2 * pairs),
        block(1, pairs),
        key_label,
        query_label,
    ]
    return column, log_total, operands


def attend_operands(operand):
    bounds, joined, rim, key_labels, query_labels = operand
    return (bounds, joined, rim, joined, rim, rim, joined, rim, key_labels, query_labels)


def attend_forward(operand):
    shard_rows = operand[1].shape[0]
    tiles = shard_rows // QT
    pairs = D // PAIR
    column, log_total, operands = attend_specs(shard_rows)
    window = pltpu.VMEM((3 * shard_rows, PAIR), jnp.bfloat16)
    return pl.pallas_call(
        attend_forward_kernel,
        grid_spec=pltpu.PrefetchScalarGridSpec(
            num_scalar_prefetch=1,
            grid=(pairs,),
            in_specs=operands,
            out_specs=[column, log_total],
            scratch_shapes=[window, window],
        ),
        out_shape=[
            jax.ShapeDtypeStruct((shard_rows, D), jnp.bfloat16),
            jax.ShapeDtypeStruct((pairs, tiles, 1, 2 * QT), jnp.float32),
        ],
        cost_estimate=pl.CostEstimate(
            flops=80000 * shard_rows * D, bytes_accessed=20 * shard_rows * D, transcendentals=0
        ),
    )(*attend_operands(operand))


def attend_backward(operand, mixed, log_totals, grad_mixed):
    shard_rows = operand[1].shape[0]
    column, log_total, operands = attend_specs(shard_rows)
    window = pltpu.VMEM((3 * shard_rows, PAIR), jnp.bfloat16)
    wide = pltpu.VMEM((3 * shard_rows, PAIR), jnp.float32)
    both = pl.BlockSpec((2, shard_rows, PAIR), lambda pair, bounds: (0, 0, pair))
    rims = pl.BlockSpec((2, 2 * shard_rows, PAIR), lambda pair, bounds: (0, 0, pair))
    return pl.pallas_call(
        attend_backward_kernel,
        grid_spec=pltpu.PrefetchScalarGridSpec(
            num_scalar_prefetch=1,
            grid=(D // PAIR,),
            in_specs=operands + [column, log_total, column],
            out_specs=[column, both, rims],
            scratch_shapes=[window, window, wide, wide],
        ),
        out_shape=[
            jax.ShapeDtypeStruct((shard_rows, D), jnp.bfloat16),
            jax.ShapeDtypeStruct((2, shard_rows, D), jnp.bfloat16),
            jax.ShapeDtypeStruct((2, 2 * shard_rows, D), jnp.bfloat16),
        ],
        cost_estimate=pl.CostEstimate(
            flops=90000 * shard_rows * D, bytes_accessed=40 * shard_rows * D, transcendentals=0
        ),
    )(*attend_operands(operand), mixed, log_totals, grad_mixed)


def attend_plan(query_start, shard_rows, starts):
    places = query_start - shard_rows + jnp.arange(3 * shard_rows, dtype=jnp.int32)
    after = starts[None, :] <= places[:, None]
    inside = after & (places[:, None] < starts[None, :] + IMG)
    counted = jnp.sum(after.astype(jnp.int32), axis=1) - 1
    owned = jnp.any(inside, axis=1)
    labels = jnp.where(owned, counted, -(2**24) - places)
    image = jnp.sum(jnp.where(inside, starts[None, :], 0), axis=1)
    own = slice(shard_rows, 2 * shard_rows)
    base = query_start - shard_rows
    first = jnp.where(owned, image, places)[own].reshape(-1, QT)[:, 0] - base
    last = jnp.where(owned, image + IMG, places + 1)[own].reshape(-1, QT)[:, -1] - base
    low = jnp.maximum(first, 0) // KT
    high = jnp.minimum((last + KT - 1) // KT, 3 * shard_rows // KT)
    bounds = jnp.stack([low, high], axis=1).reshape(-1).astype(jnp.int32)
    key_labels = jnp.broadcast_to(labels[:, None], (3 * shard_rows, PAIR))
    tiles = labels[own].reshape(-1, 1, QT)
    return bounds, key_labels, jnp.concatenate([tiles, tiles], axis=2)


def neighbours(low_going, high_going):
    count = lax.axis_size("fsdp")
    forward = [(i, i + 1) for i in range(count - 1)]
    backward = [(target, source) for source, target in forward]
    from_low = lax.ppermute(high_going, "fsdp", forward)
    from_high = lax.ppermute(low_going, "fsdp", backward)
    return from_low, from_high


def swapped(value, axis, bit):
    count = lax.axis_size(axis)
    return lax.ppermute(value, axis, [(i, i ^ bit) for i in range(count)])


def picked(value, dim, half, bit):
    size = value.shape[dim] // 2
    return lax.dynamic_slice_in_dim(value, (bit ^ half) * size, size, axis=dim)


def halved(value, dim, axis, bit):
    mine = (lax.axis_index(axis) // bit) % 2
    arrived = swapped(picked(value, dim, 1, mine), axis, bit)
    return picked(value, dim, 0, mine) + arrived


def doubled(value, dim, axis, bit):
    mine = (lax.axis_index(axis) // bit) % 2
    arrived = swapped(value, axis, bit)
    low = jnp.where(mine == 0, value, arrived)
    high = jnp.where(mine == 0, arrived, value)
    return jnp.concatenate([low, high], axis=dim)


def over_fsdp(value):
    count = lax.axis_size("fsdp")
    outer = count // 2
    rows, columns = value.shape[1:]
    value = value.reshape(outer, 2 * rows, columns)
    value = halved(value, 1, "fsdp", 1)
    bit = 2
    span = outer
    value = value.reshape(span, rows, columns)
    while span > 1:
        value = value.reshape(span // 2, 2 * rows, columns)
        value = halved(value, 1, "fsdp", bit)
        span //= 2
        bit *= 2
    return value.reshape(rows, columns)


def reduce_all(grad):
    count = lax.axis_size("fsdp")
    value = grad.astype(jnp.bfloat16).reshape(count, -1, grad.shape[1])
    value = halved(value, 1, "rep", 1)
    half = value.shape[1] // 2
    first = halved(value[:, :half], 1, "rep", 2)
    first = over_fsdp(first)
    second = over_fsdp(value[:, half:])
    first = doubled(first, 0, "rep", 2)
    second = second + swapped(second, "rep", 2)
    return doubled(jnp.concatenate([first, second], axis=0), 0, "rep", 1).astype(jnp.float32)


def body(
    tokens,
    out_grad,
    image_starts,
    first_gain,
    first_shift,
    qkv_weight,
    query_bias,
    value_bias,
    out_weight,
    out_bias,
    second_gain,
    second_shift,
    up_weight,
    up_bias,
    down_weight,
    down_bias,
):
    micro_count, shard_rows, _ = tokens.shape
    query_start = lax.axis_index("fsdp") * shard_rows

    def gathered(shard):
        rows = shard.shape[0] // lax.axis_size("rep")
        mine = lax.dynamic_slice_in_dim(shard, lax.axis_index("rep") * rows, rows, axis=0)
        return lax.all_gather(mine, ("fsdp", "rep"), axis=0, tiled=True)

    small = jnp.concatenate(
        [
            jnp.stack(
                [
                    first_gain,
                    first_shift,
                    query_bias,
                    value_bias,
                    out_bias,
                    second_gain,
                    second_shift,
                    down_bias,
                ]
            ).reshape(-1),
            up_bias,
        ]
    )
    count = lax.axis_size("fsdp")
    small = gathered(small).reshape(count, -1).astype(jnp.float32)
    part = D // count
    (
        first_gain,
        first_shift,
        query_bias,
        value_bias,
        out_bias,
        second_gain,
        second_shift,
        down_bias,
    ) = [small[:, i * part : (i + 1) * part].reshape(-1) for i in range(8)]
    up_bias = small[:, 8 * part :].reshape(-1)
    qkv_weight = gathered(qkv_weight)
    out_weight = gathered(out_weight)
    up_weight = gathered(up_weight)
    down_weight = gathered(down_weight)

    plans = [
        attend_plan(query_start, shard_rows, image_starts[micro, 0])
        for micro in range(micro_count)
    ]
    inputs = tokens.reshape(-1, D).astype(jnp.float32)
    rim_tokens = []
    for micro in range(micro_count):
        low, high = neighbours(tokens[micro], tokens[micro])
        rim_tokens.append(jnp.concatenate([low, high], axis=0))
    normed_one, factor_one = norm_stats(inputs)
    first_in = (normed_one * first_gain + first_shift).astype(jnp.bfloat16)
    joined_bias = jnp.concatenate([query_bias, jnp.zeros_like(query_bias), value_bias])
    joined = (product(first_in, qkv_weight) + joined_bias).astype(jnp.bfloat16)
    rim_normed = []
    rim_in = []
    operands = []
    mixed_parts = []
    totals_parts = []
    for micro in range(micro_count):
        normed, _ = norm_stats(rim_tokens[micro].astype(jnp.float32))
        rim_normed.append(normed)
        rim_in.append((normed * first_gain + first_shift).astype(jnp.bfloat16))
        rim = (product(rim_in[micro], qkv_weight[:, D:]) + joined_bias[D:]).astype(jnp.bfloat16)
        rows = joined[micro * shard_rows : (micro + 1) * shard_rows]
        bounds, key_labels, query_labels = plans[micro]
        operand = (bounds, rows, rim, key_labels, query_labels)
        mixed, log_totals = attend_forward(operand)
        operands.append(operand)
        mixed_parts.append(mixed)
        totals_parts.append(log_totals)
    mixed_rows = jnp.concatenate(mixed_parts, axis=0)
    middle = inputs + product(mixed_rows, out_weight) + out_bias
    normed_two, factor_two = norm_stats(middle)
    second_in = (normed_two * second_gain + second_shift).astype(jnp.bfloat16)
    hidden = product(second_in, up_weight) + up_bias
    phi = 0.5 * (1.0 + lax.erf(hidden * (2.0**-0.5)))
    active = (hidden * phi).astype(jnp.bfloat16)
    slope = phi + hidden * jnp.exp(-0.5 * hidden * hidden) * ((2.0 * jnp.pi) ** -0.5)
    layer_out = (middle + product(active, down_weight) + down_bias).astype(jnp.bfloat16)

    cotangent = out_grad.reshape(-1, D)
    grad_out = cotangent.astype(jnp.float32)
    down_grad = product_left(active, cotangent)
    down_bias_grad = jnp.sum(grad_out, axis=0)
    grad_hidden = (product_right(cotangent, down_weight) * slope).astype(jnp.bfloat16)
    up_grad = product_left(second_in, grad_hidden)
    up_bias_grad = jnp.sum(grad_hidden.astype(jnp.float32), axis=0)
    grad_second = product_right(grad_hidden, up_weight)
    second_gain_grad = jnp.sum(grad_second * normed_two, axis=0)
    second_shift_grad = jnp.sum(grad_second, axis=0)
    grad_middle = grad_out + norm_back(grad_second * second_gain, normed_two, factor_two)
    grad_branch = grad_middle.astype(jnp.bfloat16)
    out_weight_grad = product_left(mixed_rows, grad_branch)
    out_bias_grad = jnp.sum(grad_branch.astype(jnp.float32), axis=0)
    grad_mixed = product_right(grad_branch, out_weight).astype(jnp.bfloat16)
    grad_parts = []
    rim_grads = []
    from_lows = []
    from_highs = []
    rim_gain_grad = 0.0
    rim_shift_grad = 0.0
    for micro in range(micro_count):
        grad_query, grad_own, grad_rim = attend_backward(
            operands[micro],
            mixed_parts[micro],
            totals_parts[micro],
            grad_mixed[micro * shard_rows : (micro + 1) * shard_rows],
        )
        grad_parts.append(jnp.concatenate([grad_query, grad_own[0], grad_own[1]], axis=1))
        grad_rim = jnp.concatenate([grad_rim[0], grad_rim[1]], axis=1)
        rim_grads.append(grad_rim)
        grad_rim_in = product_right(grad_rim, qkv_weight[:, D:])
        rim_gain_grad += jnp.sum(grad_rim_in * rim_normed[micro], axis=0)
        rim_shift_grad += jnp.sum(grad_rim_in, axis=0)
        returned = grad_rim_in.astype(jnp.bfloat16)
        from_low, from_high = neighbours(returned[:shard_rows], returned[shard_rows:])
        from_lows.append(from_low)
        from_highs.append(from_high)
    grad_joined = jnp.concatenate(grad_parts, axis=0)
    grad_rim = jnp.concatenate(rim_grads, axis=0)
    query_grad = product_left(first_in, grad_joined[:, :D]).astype(jnp.bfloat16)
    key_value_grad = product_left(
        jnp.concatenate([first_in] + rim_in, axis=0),
        jnp.concatenate([grad_joined[:, D:], grad_rim], axis=0),
    ).astype(jnp.bfloat16)
    qkv_grad = jnp.concatenate([query_grad, key_value_grad], axis=1)
    query_bias_grad = jnp.sum(grad_joined[:, :D].astype(jnp.float32), axis=0)
    value_bias_grad = jnp.sum(grad_joined[:, 2 * D :].astype(jnp.float32), axis=0) + jnp.sum(
        grad_rim[:, D:].astype(jnp.float32), axis=0
    )
    grad_first = product_right(grad_joined, qkv_weight)
    first_gain_grad = jnp.sum(grad_first * normed_one, axis=0) + rim_gain_grad
    first_shift_grad = jnp.sum(grad_first, axis=0) + rim_shift_grad
    grad_first = grad_first + (
        jnp.concatenate(from_lows, axis=0).astype(jnp.float32)
        + jnp.concatenate(from_highs, axis=0).astype(jnp.float32)
    )
    tokens_grad = (
        grad_middle + norm_back(grad_first * first_gain, normed_one, factor_one)
    ).astype(jnp.bfloat16)

    small_grads = [
        first_gain_grad,
        first_shift_grad,
        query_bias_grad,
        value_bias_grad,
        out_bias_grad,
        second_gain_grad,
        second_shift_grad,
        down_bias_grad,
        up_bias_grad,
    ]
    packed = jnp.concatenate([grad.reshape(count, -1) for grad in small_grads], axis=1)
    width = packed.shape[1]
    lanes = -(-width // 2048) * 128
    packed = jnp.pad(packed, ((0, 0), (0, 16 * lanes - width)))
    packed = reduce_all(packed.reshape(count * 16, lanes)).reshape(-1)
    smalls = [packed[i * part : (i + 1) * part] for i in range(8)] + [packed[8 * part : width]]
    down_grad = reduce_all(down_grad)
    up_grad = reduce_all(up_grad)
    out_weight_grad = reduce_all(out_weight_grad)
    qkv_grad = reduce_all(qkv_grad)
    return (
        layer_out.reshape(tokens.shape),
        tokens_grad.reshape(tokens.shape),
        smalls[0],
        smalls[1],
        qkv_grad,
        smalls[2],
        smalls[3],
        out_weight_grad,
        smalls[4],
        smalls[5],
        smalls[6],
        up_grad,
        smalls[8],
        down_grad,
        smalls[7],
    )


def solution(mesh):
    placed = (
        P(None, ("rep", "fsdp"), None),
        P(None, ("rep", "fsdp"), None),
        P(None, "rep", None),
        P("fsdp"),
        P("fsdp"),
        P("fsdp", None),
        P("fsdp"),
        P("fsdp"),
        P("fsdp", None),
        P("fsdp"),
        P("fsdp"),
        P("fsdp"),
        P("fsdp", None),
        P("fsdp"),
        P("fsdp", None),
        P("fsdp"),
    )
    return jax.shard_map(
        body,
        mesh=mesh,
        in_specs=placed,
        out_specs=(
            P(None, ("rep", "fsdp"), None),
            P(None, ("rep", "fsdp"), None),
            P("fsdp"),
            P("fsdp"),
            P("fsdp", None),
            P("fsdp"),
            P("fsdp"),
            P("fsdp", None),
            P("fsdp"),
            P("fsdp"),
            P("fsdp"),
            P("fsdp", None),
            P("fsdp"),
            P("fsdp", None),
            P("fsdp"),
        ),
        check_vma=False,
    )
```
